32 devices in a mesh: grp: 2 (over y), tok: 4 (over z), sec: 2 (over core), ch: 2 (over x).
Axes of the slice: x: 2, y: 2, z: 4, core: 2. Of those that a mesh axis runs over, the one named last changes fastest.
Arguments:
- features: bfloat16 [4096, 2048], P('ch', ('grp', 'tok', 'sec')), parts along dimension 1, may hold values from -6 to 6
- gate_one: bfloat16 [4096, 2048], P('ch', ('grp', 'tok', 'sec')), parts along dimension 1, may hold values from -6 to 6
- taps_one: bfloat16 [4096, 128], P('ch'), may hold values from -0.5 to 0.5
- long_filter: bfloat16 [4096, 1024], P('ch', ('tok', 'sec')), may hold values from -0.1875 to 0.1875
- skip_gain: float32 [4096], P('ch'), may hold values from 0.5 to 1.5
- taps_two: bfloat16 [4096, 128], P('ch'), may hold values from -0.5 to 0.5
- gate_two: bfloat16 [4096, 2048], P('ch', ('grp', 'tok', 'sec')), parts along dimension 1, may hold values from -6 to 6
Outputs:
- mixed_out: bfloat16 [4096, 2048], P('ch', ('grp', 'tok', 'sec')), parts along dimension 1
The draws below stay inside these ranges and needn't reach their ends.
There are 2 independent parts, one for each index of `grp`. The reference program is written for one: setup_inputs(seed, part) draws one part's arguments, and reference() takes and returns one part's arrays. A program takes and returns all parts, laid end to end along the dimension named above; an argument that names none is the same for every part. Nothing has to cross between parts.
All inputs are finite; a program needn't handle non-finite values.
Results may differ from the reference program's by a relative error of at most 0.0057.
Values may be sent and summed in bfloat16 or wider, within the bound.
No kernel may reach another device: no remote copies, remote signals or barrier semaphores. Data moves between devices by JAX's collectives and lax.ppermute only.
A program may use at most 192 MiB of HBM per device.

```python
import jax
import jax.numpy as jnp
from jax import lax

D = 4096
TAPS = 128
SEQ = 1024


def block_scale(own_key, extent, cuts, smallest, top_value):
    level = 1.0
    for axis_at, blocks in cuts:
        draws = jax.random.uniform(jax.random.fold_in(jax.random.fold_in(own_key, 6), axis_at), (blocks,), jnp.float32, smallest / len(cuts), top_value / len(cuts))
        level = level * jnp.repeat(jnp.exp(draws), extent[axis_at] // blocks).reshape((-1,) + (1,) * (len(extent) - 1 - axis_at))
    return level


def centred(rng, dims, scale, bound, cuts=(), dtype=jnp.bfloat16):
    values = scale * jax.random.normal(rng, dims, jnp.float32)
    if cuts:
        values = values * block_scale(rng, dims, cuts, -0.22, 0.18)
    return jnp.clip(values, -bound, bound).astype(dtype)


def setup_inputs(seed: int = 0, part: int = 0) -> dict:
    key_of = jax.random.split(jax.random.key(seed), 8)
    part_splits = jax.random.split(jax.random.fold_in(key_of[7], part), 8)
    return {
        "features": centred(part_splits[0], (D, SEQ), 1.0, 6.0, ((0, 2), (1, 8))),
        "gate_one": centred(part_splits[1], (D, SEQ), 1.0, 6.0, ((0, 2), (1, 8))),
        "taps_one": centred(key_of[2], (D, TAPS), TAPS ** -0.5, 0.5, ((0, 2),)),
        "long_filter": centred(key_of[3], (D, SEQ), SEQ ** -0.5, 0.1875, ((0, 2), (1, 8))),
        "skip_gain": jnp.clip(0.5 + 1.0 * jax.random.uniform(key_of[4], (D,), jnp.float32) ** block_scale(key_of[4], (D,), ((0, 2),), -0.2, 0.2), 0.5, 1.5),
        "taps_two": centred(key_of[5], (D, TAPS), TAPS ** -0.5, 0.5, ((0, 2),)),
        "gate_two": centred(part_splits[6], (D, SEQ), 1.0, 6.0, ((0, 2), (1, 8))),
    }


def causal_conv(signal, kernel_taps):
    padded = jnp.pad(signal.astype(jnp.float32), ((0, 0), (TAPS - 1, 0)))
    taps_wide = kernel_taps.astype(jnp.float32)
    length = signal.shape[1]

    def add_tap(step, total):
        offset = (TAPS - 1 - step).astype(jnp.int32)
        shifted = lax.dynamic_slice_in_dim(padded, offset, length, 1)
        weight = lax.dynamic_slice_in_dim(taps_wide, jnp.asarray(step).astype(jnp.int32), 1, 1)
        return total + weight * shifted

    return lax.fori_loop(0, TAPS, add_tap, jnp.zeros(signal.shape, jnp.float32))


def long_block(pieces):
    signal, filter_row, gain_row = pieces
    total = 2 * SEQ
    signal_wide = signal.astype(jnp.float32)
    spectrum = jnp.fft.rfft(signal_wide, n=total) * jnp.fft.rfft(filter_row.astype(jnp.float32), n=total)
    conv_out = jnp.fft.irfft(spectrum, n=total)[:, :SEQ]
    return (conv_out + gain_row[:, None] * signal_wide).astype(jnp.bfloat16)


def reference(features, gate_one, taps_one, long_filter, skip_gain, taps_two, gate_two):
    mixed_one = (causal_conv(features, taps_one) * gate_one.astype(jnp.float32)).astype(jnp.bfloat16)
    blocks = D // 256
    long_out = lax.map(long_block, (mixed_one.reshape(blocks, 256, SEQ), long_filter.reshape(blocks, 256, SEQ), skip_gain.reshape(blocks, 256))).reshape(D, SEQ)
    return (causal_conv(long_out, taps_two) * gate_two.astype(jnp.float32)).astype(jnp.bfloat16)
```

```python
import functools
import math

import jax
import jax.numpy as jnp
import numpy as np
from jax import lax
from jax.experimental import pallas as pl
from jax.experimental.pallas import tpu as pltpu
from jax.sharding import PartitionSpec as P

AXES = ("tok", "sec")
F32 = jnp.float32
BF16 = jnp.bfloat16


def split_const(matrix):
    hi = matrix.astype(np.float32).astype(jnp.bfloat16)
    lo = (matrix - hi.astype(np.float64)).astype(np.float32).astype(jnp.bfloat16)
    return hi, lo


def tables(block):
    length = 2 * block
    sample = np.arange(length)[:, None]
    freq = np.arange(block)[None, :]
    turns = (sample * (2 * freq + 1)) % (2 * length)
    angle = turns * (math.pi / length)
    forward = np.concatenate([np.cos(angle), -np.sin(angle)], axis=1)
    hi, lo = split_const(forward)
    top = np.concatenate([hi[:block], lo[:block]], axis=0)
    back = forward[block:].T / block
    back_hi, back_lo = split_const(back)
    both = np.concatenate([back_hi, back_lo], axis=1)
    return tuple(jnp.asarray(t) for t in (hi, lo, top, both))


def mm(left, right):
    return jnp.dot(left, right, preferred_element_type=F32)


def window_spectrum(before, here, hi, lo):
    window = jnp.concatenate([before, here], axis=1)
    return mm(window, hi) + mm(window, lo)


def block_spectrum(rows, top):
    return mm(jnp.concatenate([rows, rows], axis=1), top)


def two_parts(value):
    hi = value.astype(BF16)
    return hi, (value - hi.astype(F32)).astype(BF16)


def times(left, right):
    n = left.shape[-1] // 2
    lr, li, rr, ri = left[:, :n], left[:, n:], right[:, :n], right[:, n:]
    return jnp.concatenate([lr * rr - li * ri, lr * ri + li * rr], axis=1)


def valid_part(spectrum, both):
    n = both.shape[1] // 2
    hi, lo = two_parts(spectrum)
    wide = mm(hi, both)
    return wide[:, :n] + wide[:, n:] + mm(lo, both[:, :n])


def rows_at(index, rows):
    return pl.ds(pl.multiple_of(index * rows, rows), rows)


def first_kernel(shards, me_ref, x_ref, halo_ref, gate_ref, taps_ref, hi_ref, lo_ref, top_ref, both_ref, *outs):
    rows = outs[0].shape[0]
    me = me_ref[0]
    hi, lo, top, both = hi_ref[...], lo_ref[...], top_ref[...], both_ref[...]
    for k in range(shards):
        at = rows_at(me ^ k, rows)
        spectrum = window_spectrum(halo_ref[at, :], x_ref[at, :], hi, lo)
        taps = block_spectrum(taps_ref[at, :], top)
        conv = valid_part(times(spectrum, taps), both)
        outs[k][...] = (conv * gate_ref[at, :].astype(F32)).astype(BF16)


def filter_kernel(shards, me_ref, mine_ref, other_ref, taps_ref, skip_ref, hi_ref, lo_ref, top_ref, both_ref, out_ref, lags, taps_hat):
    half = mine_ref.shape[1]
    me, group = me_ref[0], me_ref[1]
    hi, lo, top, both = hi_ref[...], lo_ref[...], top_ref[...], both_ref[...]
    lags[0] = jnp.zeros(lags.shape[1:], BF16)
    for k in range(shards):
        lags[(me ^ k) + 1, rows_at(group, half), :] = mine_ref[k]
        lags[(me ^ k) + 1, rows_at(1 - group, half), :] = other_ref[k]
    taps_hat[...] = block_spectrum(taps_ref[...], top)
    for m in range(shards):
        spectrum = window_spectrum(lags[m], lags[m + 1], hi, lo)
        joined = valid_part(times(spectrum, taps_hat[...]), both)
        part_hi, part_lo = two_parts(joined)
        n = part_hi.shape[1]
        result = block_spectrum(part_hi, top) + mm(part_lo, top[:n])
        if m == 0:
            result = result + skip_ref[...] * taps_hat[...]
        out_ref[m] = result


def long_kernel(shards, me_ref, *refs):
    pieces = refs[:shards]
    filt_ref, hi_ref, lo_ref, both_ref = refs[shards : shards + 4]
    outs = refs[shards + 4 : 2 * shards + 4]
    signal, spectra, sums = refs[2 * shards + 4 :]
    rows, block = pieces[0].shape
    me = me_ref[0]
    hi, lo, both = hi_ref[...], lo_ref[...], both_ref[...]
    signal[0] = jnp.zeros((rows, block), BF16)
    for k in range(shards):
        signal[(me ^ k) + 1] = pieces[k][...]
    for j in range(shards):
        spectra[j] = window_spectrum(signal[j], signal[j + 1], hi, lo)
    tile = 8

    def body(i, carry):
        at = pl.ds(pl.multiple_of(i * tile, tile), tile)
        fr = [filt_ref[m, at, :block] for m in range(shards)]
        fi = [filt_ref[m, at, block:] for m in range(shards)]
        sr = [spectra[m, at, :block] for m in range(shards)]
        si = [spectra[m, at, block:] for m in range(shards)]
        for j in range(shards):
            re = fr[0] * sr[j] - fi[0] * si[j]
            im = fr[0] * si[j] + fi[0] * sr[j]
            for m in range(1, j + 1):
                re = re + (fr[m] * sr[j - m] - fi[m] * si[j - m])
                im = im + (fr[m] * si[j - m] + fi[m] * sr[j - m])
            sums[j, at, :block] = re
            sums[j, at, block:] = im
        return carry

    lax.fori_loop(0, rows // tile, body, 0)
    for k in range(shards):
        outs[k][...] = valid_part(sums[me ^ k], both).astype(BF16)


def last_kernel(shards, me_ref, *refs):
    pieces, gate_ref, out_ref = refs[:shards], refs[shards], refs[shards + 1]
    rows = pieces[0].shape[0]
    me = me_ref[0]
    for k in range(shards):
        at = rows_at(me ^ k, rows)
        out_ref[at, :] = (pieces[k][...].astype(F32) * gate_ref[at, :].astype(F32)).astype(BF16)


def call(kernel, inputs, out_shape, scratch=(), flops=0, name=None):
    vmem = pl.BlockSpec(memory_space=pltpu.VMEM)
    many = isinstance(out_shape, (list, tuple))
    moved = sum(math.prod(a.shape) * a.dtype.itemsize for a in inputs)
    return pl.pallas_call(
        kernel,
        out_shape=out_shape,
        in_specs=[pl.BlockSpec(memory_space=pltpu.SMEM)] + [vmem] * (len(inputs) - 1),
        out_specs=[vmem] * len(out_shape) if many else vmem,
        scratch_shapes=list(scratch),
        compiler_params=pltpu.CompilerParams(vmem_limit_bytes=28 * 1024 * 1024),
        cost_estimate=pl.CostEstimate(flops=flops, bytes_accessed=moved, transcendentals=0),
        name=name,
    )(*inputs)


def on_device(features, gate_one, taps_one, long_filter, skip_gain, taps_two, gate_two):
    shards = lax.axis_size(AXES)
    groups = lax.axis_size("grp")
    assert shards & (shards - 1) == 0 and groups == 2
    channels, block = features.shape
    assert taps_one.shape[1] == block and taps_two.shape[1] == block
    narrow = channels // shards
    half = narrow // groups
    hi, lo, top, both = tables(block)
    me = lax.axis_index(AXES)
    group = lax.axis_index("grp")
    place = jnp.stack([me, group]).astype(jnp.int32)
    flops = 2 * channels * 256 * 256

    def swapped(piece, k):
        return lax.ppermute(piece, AXES, [(i, i ^ k) for i in range(shards)])

    halo = lax.ppermute(features, AXES, [(i, i + 1) for i in range(shards - 1)])

    by_owner = long_filter.reshape(shards, groups, half, block)
    lags = [
        lax.dynamic_slice(by_owner, (me ^ k, group, 0, 0), (1, 1, half, block)).reshape(half, block)
        for k in range(shards)
    ]
    lags = [lags[0]] + [swapped(lags[k], k) for k in range(1, shards)]
    mine = jnp.stack(lags)
    other = lax.ppermute(mine, "grp", [(0, 1), (1, 0)])

    piece = jax.ShapeDtypeStruct((narrow, block), BF16)
    mixed = call(
        functools.partial(first_kernel, shards),
        (place, features, halo, gate_one, taps_one, hi, lo, top, both),
        [piece] * shards,
        flops=6 * flops,
        name="first",
    )
    mixed = [mixed[0]] + [swapped(mixed[k], k) for k in range(1, shards)]

    taps_local = lax.dynamic_slice_in_dim(taps_two, me * narrow, narrow)
    skip_local = lax.dynamic_slice_in_dim(skip_gain, me * narrow, narrow)[:, None]
    joined = call(
        functools.partial(filter_kernel, shards),
        (place, mine, other, taps_local, skip_local, hi, lo, top, both),
        jax.ShapeDtypeStruct((shards, narrow, 2 * block), F32),
        scratch=[
            pltpu.VMEM((shards + 1, narrow, block), BF16),
            pltpu.VMEM((narrow, 2 * block), F32),
        ],
        flops=6 * flops,
        name="filter",
    )
    result = call(
        functools.partial(long_kernel, shards),
        (place, *mixed, joined, hi, lo, both),
        [piece] * shards,
        scratch=[
            pltpu.VMEM((shards + 1, narrow, block), BF16),
            pltpu.VMEM((shards, narrow, 2 * block), F32),
            pltpu.VMEM((shards, narrow, 2 * block), F32),
        ],
        flops=6 * flops,
        name="long",
    )
    result = [result[0]] + [swapped(result[k], k) for k in range(1, shards)]
    return call(
        functools.partial(last_kernel, shards),
        (place, *result, gate_two),
        jax.ShapeDtypeStruct((channels, block), BF16),
        flops=channels * block,
        name="last",
    )


def solution(mesh):
    in_specs = (
        P("ch", ("grp", "tok", "sec")),
        P("ch", ("grp", "tok", "sec")),
        P("ch", None),
        P("ch", ("tok", "sec")),
        P("ch"),
        P("ch", None),
        P("ch", ("grp", "tok", "sec")),
    )
    out_specs = P("ch", ("grp", "tok", "sec"))
    return jax.shard_map(
        on_device, mesh=mesh, in_specs=in_specs, out_specs=out_specs, check_vma=False
    )
```

```python
import functools
import math

import jax
import jax.numpy as jnp
import numpy as np
from jax import lax
from jax.experimental import pallas as pl
from jax.experimental.pallas import tpu as pltpu
from jax.sharding import PartitionSpec as P


AXES = ("tok", "sec")
F32 = jnp.float32
BF16 = jnp.bfloat16


def split_const(matrix):
    hi = matrix.astype(np.float32).astype(jnp.bfloat16)
    lo = (matrix - hi.astype(np.float64)).astype(np.float32).astype(jnp.bfloat16)
    return hi, lo


def tables(block):
    length = 2 * block
    sample = np.arange(length)[:, None]
    freq = np.arange(block)[None, :]
    turns = (sample * (2 * freq + 1)) % (2 * length)
    angle = turns * (math.pi / length)
    forward = np.concatenate([np.cos(angle), -np.sin(angle)], axis=1)
    hi, lo = split_const(forward)
    top = np.concatenate([hi[:block], lo[:block]], axis=0)
    back = forward[block:].T / block
    back_hi, back_lo = split_const(back)
    both = np.concatenate([back_hi, back_lo], axis=1)
    return jnp.asarray(np.concatenate([hi, lo, top, both], axis=0))


def parts_of(table_ref):
    n = table_ref.shape[1]
    return tuple(table_ref[i * n : (i + 1) * n, :] for i in range(4))


def mm(left, right):
    return jnp.dot(left, right, preferred_element_type=F32)


def window_spectrum(before, here, hi, lo):
    window = jnp.concatenate([before, here], axis=1)
    return mm(window, hi) + mm(window, lo)


def block_spectrum(rows, top):
    return mm(jnp.concatenate([rows, rows], axis=1), top)


def two_parts(value):
    hi = value.astype(BF16)
    return hi, (value - hi.astype(F32)).astype(BF16)


def times(left, right):
    n = left.shape[-1] // 2
    lr, li, rr, ri = left[:, :n], left[:, n:], right[:, :n], right[:, n:]
    return jnp.concatenate([lr * rr - li * ri, lr * ri + li * rr], axis=1)


def valid_part(spectrum, both):
    n = both.shape[1] // 2
    hi, lo = two_parts(spectrum)
    wide = mm(hi, both)
    return wide[:, :n] + wide[:, n:] + mm(lo, both[:, :n])


def rows_at(index, rows):
    return pl.ds(pl.multiple_of(index * rows, rows), rows)


def first_kernel(which, me_ref, halo_ref, table_ref, *refs):
    count = len(which)
    outs = refs[3 * count :]
    rows = outs[0].shape[0]
    me = me_ref[0]
    hi, lo, top, both = parts_of(table_ref)
    for i, k in enumerate(which):
        x_ref, gate_ref, taps_ref = refs[3 * i : 3 * i + 3]
        spectrum = window_spectrum(halo_ref[rows_at(me ^ k, rows), :], x_ref[...], hi, lo)
        taps = block_spectrum(taps_ref[...], top)
        conv = valid_part(times(spectrum, taps), both)
        outs[i][...] = (conv * gate_ref[...].astype(F32)).astype(BF16)


def filter_kernel(shards, me_ref, mine_ref, other_ref, taps_ref, skip_ref, table_ref, out_ref, lags, taps_hat):
    half = mine_ref.shape[1]
    me, group = me_ref[0], me_ref[1]
    hi, lo, top, both = parts_of(table_ref)
    lags[0] = jnp.zeros(lags.shape[1:], BF16)
    for k in range(shards):
        lags[(me ^ k) + 1, rows_at(group, half), :] = mine_ref[k]
        lags[(me ^ k) + 1, rows_at(1 - group, half), :] = other_ref[k]
    taps_hat[...] = block_spectrum(taps_ref[...], top)
    for m in range(shards):
        spectrum = window_spectrum(lags[m], lags[m + 1], hi, lo)
        joined = valid_part(times(spectrum, taps_hat[...]), both)
        part_hi, part_lo = two_parts(joined)
        n = part_hi.shape[1]
        result = block_spectrum(part_hi, top) + mm(part_lo, top[:n])
        if m == 0:
            result = result + skip_ref[...] * taps_hat[...]
        out_ref[m] = result


def lead_kernel(shards, lead, me_ref, *refs):
    pieces = refs[:shards]
    filt_ref, table_ref, out_ref, spectra, signal, total = refs[shards:]
    rows, block = pieces[0].shape
    me = me_ref[0]
    hi, lo, _, both = parts_of(table_ref)
    signal[0] = jnp.zeros((rows, block), BF16)
    for k in range(shards):
        signal[(me ^ k) + 1] = pieces[k][...]
    for j in range(shards):
        spectra[j] = window_spectrum(signal[j], signal[j + 1], hi, lo)
    j = me ^ lead
    tile = min(64, rows)

    def row_tile(i, carry):
        at = pl.ds(pl.multiple_of(i * tile, tile), tile)

        def term(m, sums):
            fr, fi = filt_ref[m, at, :block], filt_ref[m, at, block:]
            sr, si = spectra[j - m, at, :block], spectra[j - m, at, block:]
            return sums[0] + (fr * sr - fi * si), sums[1] + (fr * si + fi * sr)

        zero = jnp.zeros((tile, block), F32)
        re, im = lax.fori_loop(0, j + 1, term, (zero, zero))
        total[at, :block] = re
        total[at, block:] = im
        return carry

    lax.fori_loop(0, rows // tile, row_tile, 0)
    out_ref[...] = valid_part(total[...], both).astype(BF16)


def long_kernel(shards, which, me_ref, filt_ref, spectra, table_ref, *refs):
    outs, sums = refs[:-1], refs[-1]
    rows, block = outs[0].shape
    me = me_ref[0]
    both = parts_of(table_ref)[3]
    tile = 8

    def body(i, carry):
        at = pl.ds(pl.multiple_of(i * tile, tile), tile)
        fr = [filt_ref[m, at, :block] for m in range(shards)]
        fi = [filt_ref[m, at, block:] for m in range(shards)]
        sr = [spectra[m, at, :block] for m in range(shards)]
        si = [spectra[m, at, block:] for m in range(shards)]
        for j in range(shards):
            re = fr[0] * sr[j] - fi[0] * si[j]
            im = fr[0] * si[j] + fi[0] * sr[j]
            for m in range(1, j + 1):
                re = re + (fr[m] * sr[j - m] - fi[m] * si[j - m])
                im = im + (fr[m] * si[j - m] + fi[m] * sr[j - m])
            sums[j, at, :block] = re
            sums[j, at, block:] = im
        return carry

    lax.fori_loop(0, rows // tile, body, 0)
    for k, out_ref in zip(which, outs):
        out_ref[...] = valid_part(sums[me ^ k], both).astype(BF16)


def last_kernel(order, me_ref, *refs):
    count = len(order)
    pieces, gates = refs[:count], refs[count : 2 * count]
    out_ref, made, sems = refs[2 * count :]
    rows = pieces[0].shape[0]
    me = me_ref[0]
    copies = []
    for i, k in enumerate(order):
        at = rows_at(me ^ k, rows)
        made[i] = (pieces[i][...].astype(F32) * gates[i][...].astype(F32)).astype(BF16)
        copies.append(pltpu.make_async_copy(made.at[i], out_ref.at[at, :], sems.at[i]))
        copies[-1].start()
    for copy in copies:
        copy.wait()


VMEM = pl.BlockSpec(memory_space=pltpu.VMEM)
HBM = pl.BlockSpec(memory_space=pltpu.HBM)


def size_of(arrays):
    return sum(math.prod(a.shape) * a.dtype.itemsize for a in arrays)


def call(kernel, inputs, out_shape, scratch=(), flops=0, in_space=VMEM, out_space=VMEM, limit=28 * 2**20):
    moved = size_of(inputs)
    many = isinstance(out_shape, (list, tuple))
    return pl.pallas_call(
        kernel,
        out_shape=out_shape,
        in_specs=[pl.BlockSpec(memory_space=pltpu.SMEM)] + [in_space] * (len(inputs) - 1),
        out_specs=[out_space] * len(out_shape) if many else out_space,
        scratch_shapes=list(scratch),
        compiler_params=pltpu.CompilerParams(vmem_limit_bytes=limit),
        cost_estimate=pl.CostEstimate(flops=flops, bytes_accessed=moved, transcendentals=0),
    )(*inputs)


def far_first(shards):
    order = []
    step = shards // 2
    while step:
        order += list(range(step, 2 * step))
        step //= 2
    return order


def stages(features, gate_one, taps_one, long_filter, skip_gain, taps_two, gate_two):
    shards = lax.axis_size(AXES)
    groups = lax.axis_size("grp")
    assert shards & (shards - 1) == 0 and groups == 2
    channels, block = features.shape
    assert taps_one.shape[1] == block and taps_two.shape[1] == block
    narrow = channels // shards
    half = narrow // groups
    me = lax.axis_index(AXES)
    place = jnp.stack([me, lax.axis_index("grp")]).astype(jnp.int32)
    flops = 2 * channels * 256 * 256
    order = far_first(shards)
    lead = order[0]
    rest = order[1:] + [0]

    def swapped(piece, k):
        if k == 0:
            return piece
        return lax.ppermute(piece, AXES, [(i, i ^ k) for i in range(shards)])

    halo = lax.ppermute(features, AXES, [(i, i + 1) for i in range(shards - 1)])

    def rows_for(array, k):
        return lax.dynamic_slice_in_dim(array, (me ^ k) * narrow, narrow)

    table = tables(block)
    by_owner = long_filter.reshape(shards, groups, half, block)
    group = lax.axis_index("grp")
    lags = [
        lax.dynamic_slice(by_owner, (me ^ k, group, 0, 0), (1, 1, half, block)).reshape(half, block)
        for k in range(shards)
    ]
    mine = jnp.stack([swapped(lags[k], k) for k in range(shards)])
    other = lax.ppermute(mine, "grp", [(0, 1), (1, 0)])

    piece = jax.ShapeDtypeStruct((narrow, block), BF16)

    def operands(which):
        cuts = []
        for k in which:
            cuts += [rows_for(features, k), rows_for(gate_one, k), rows_for(taps_one, k)]
        return (place, halo, table, *cuts)

    (front,) = call(functools.partial(first_kernel, [lead]), operands([lead]), [piece], flops=flops)
    others = call(functools.partial(first_kernel, rest), operands(rest), [piece] * len(rest), flops=6 * flops)
    mixed = {k: swapped(p, k) for k, p in zip([lead] + rest, [front] + list(others))}

    skip_late, taps_late, gate_late, _ = lax.optimization_barrier((skip_gain, taps_two, gate_two, others[0]))
    skip_local = rows_for(skip_late, 0)[:, None]
    taps_local = rows_for(taps_late, 0)
    spectrum = jax.ShapeDtypeStruct((shards, narrow, 2 * block), F32)
    joined = call(
        functools.partial(filter_kernel, shards),
        (place, mine, other, taps_local, skip_local, table),
        spectrum,
        scratch=[
            pltpu.VMEM((shards + 1, narrow, block), BF16),
            pltpu.VMEM((narrow, 2 * block), F32),
        ],
        flops=6 * flops,
    )
    front, spectra = call(
        functools.partial(lead_kernel, shards, lead),
        (place, *[mixed[k] for k in range(shards)], joined, table),
        [piece, spectrum],
        scratch=[
            pltpu.VMEM((shards + 1, narrow, block), BF16),
            pltpu.VMEM((narrow, 2 * block), F32),
        ],
        flops=3 * flops,
    )
    others = call(
        functools.partial(long_kernel, shards, rest),
        (place, joined, spectra, table),
        [piece] * len(rest),
        scratch=[pltpu.VMEM((shards, narrow, 2 * block), F32)],
        flops=3 * flops,
    )
    result = {k: swapped(p, k) for k, p in zip([lead] + rest, [front] + list(others))}
    ready = [0] + order[::-1]
    return call(
        functools.partial(last_kernel, ready),
        (place, *[result[k] for k in ready], *[rows_for(gate_late, k) for k in ready]),
        jax.ShapeDtypeStruct((channels, block), BF16),
        scratch=[
            pltpu.VMEM((shards, narrow, block), BF16),
            pltpu.SemaphoreType.DMA((shards,)),
        ],
        flops=channels * block,
        out_space=HBM,
    )


def solution(mesh):
    in_specs = (
        P("ch", ("grp", "tok", "sec")),
        P("ch", ("grp", "tok", "sec")),
        P("ch", None),
        P("ch", ("tok", "sec")),
        P("ch"),
        P("ch", None),
        P("ch", ("grp", "tok", "sec")),
    )
    out_specs = P("ch", ("grp", "tok", "sec"))
    return jax.shard_map(stages, mesh=mesh, in_specs=in_specs, out_specs=out_specs, check_vma=False)
```

```python
import functools
import math

import jax
import jax.numpy as jnp
import numpy as np
from jax import lax
from jax.experimental import pallas as pl
from jax.experimental.pallas import tpu as pltpu
from jax.sharding import PartitionSpec as P


AXES = ("tok", "sec")
F32 = jnp.float32
BF16 = jnp.bfloat16


def split_const(matrix):
    hi = matrix.astype(np.float32).astype(jnp.bfloat16)
    lo = (matrix - hi.astype(np.float64)).astype(np.float32).astype(jnp.bfloat16)
    return hi, lo


def tables(block):
    length = 2 * block
    sample = np.arange(length)[:, None]
    freq = np.arange(block)[None, :]
    turns = (sample * (2 * freq + 1)) % (2 * length)
    angle = turns * (math.pi / length)
    forward = np.concatenate([np.cos(angle), -np.sin(angle)], axis=1)
    hi, lo = split_const(forward)
    top = np.concatenate([hi[:block], lo[:block]], axis=0)
    back = forward[block:].T / block
    back_hi, back_lo = split_const(back)
    both = np.concatenate([back_hi, back_lo], axis=1)
    return jnp.asarray(np.concatenate([hi, lo, top, both], axis=0))


def parts_of(table_ref):
    n = table_ref.shape[1]
    return tuple(table_ref[i * n : (i + 1) * n, :] for i in range(4))


def mm(left, right):
    return jnp.dot(left, right, preferred_element_type=F32)


def window_spectrum(before, here, hi, lo):
    window = jnp.concatenate([before, here], axis=1)
    return mm(window, hi) + mm(window, lo)


def block_spectrum(rows, top):
    return mm(jnp.concatenate([rows, rows], axis=1), top)


def two_parts(value):
    hi = value.astype(BF16)
    return hi, (value - hi.astype(F32)).astype(BF16)


def times(left, right):
    n = left.shape[-1] // 2
    lr, li, rr, ri = left[:, :n], left[:, n:], right[:, :n], right[:, n:]
    return jnp.concatenate([lr * rr - li * ri, lr * ri + li * rr], axis=1)


def valid_part(spectrum, both):
    n = both.shape[1] // 2
    hi, lo = two_parts(spectrum)
    wide = mm(hi, both)
    return wide[:, :n] + wide[:, n:] + mm(lo, both[:, :n])


def rows_at(index, rows):
    return pl.ds(pl.multiple_of(index * rows, rows), rows)


def prep_kernel(shards, table_ref, *refs):
    own_hat, taps_hat = refs[2 * shards :]
    hi, lo, top, _ = parts_of(table_ref)
    n = hi.shape[0] // 2
    bottom = jnp.concatenate([hi[n:], lo[n:]], axis=0)
    for k in range(shards):
        own_hat[k] = block_spectrum(refs[2 * k][...], bottom)
        taps_hat[k] = block_spectrum(refs[2 * k + 1][...], top)


def first_kernel(which, me_ref, halo_ref, table_ref, own_hat, taps_hat, *refs):
    count = len(which)
    gates, outs = refs[:count], refs[count:]
    rows = outs[0].shape[0]
    me = me_ref[0]
    _, _, top, both = parts_of(table_ref)
    for i, k in enumerate(which):
        spectrum = own_hat[k] + block_spectrum(halo_ref[rows_at(me ^ k, rows), :], top)
        conv = valid_part(times(spectrum, taps_hat[k]), both)
        outs[i][...] = (conv * gates[i][...].astype(F32)).astype(BF16)


def filter_kernel(toks, me_ref, held_ref, first_ref, second_ref, taps_ref, skip_ref, table_ref, out_ref, lags, taps_hat):
    tok, sec, group = me_ref[1], me_ref[2], me_ref[3]
    hi, lo, top, both = parts_of(table_ref)
    lags[0] = jnp.zeros(lags.shape[1:], BF16)

    def fill(same_ref, other_ref):
        for k in range(toks):
            at = (tok ^ k) * 2 + 1
            lags[at + sec] = same_ref[k]
            lags[at + 1 - sec] = other_ref[k]

    @pl.when(sec == group)
    def _():
        fill(held_ref, first_ref)

    @pl.when(sec != group)
    def _():
        fill(first_ref, second_ref)

    taps_hat[...] = block_spectrum(taps_ref[...], top)
    for m in range(2 * toks):
        spectrum = window_spectrum(lags[m], lags[m + 1], hi, lo)
        joined = valid_part(times(spectrum, taps_hat[...]), both)
        part_hi, part_lo = two_parts(joined)
        n = part_hi.shape[1]
        result = block_spectrum(part_hi, top) + mm(part_lo, top[:n])
        if m == 0:
            result = result + skip_ref[...] * taps_hat[...]
        out_ref[m] = result


def one_block(j, filt_ref, spectra, both, out_ref, total):
    rows, block = out_ref.shape
    tile = min(64, rows)

    def row_tile(i, carry):
        at = pl.ds(pl.multiple_of(i * tile, tile), tile)

        def term(m, sums):
            fr, fi = filt_ref[m, at, :block], filt_ref[m, at, block:]
            sr, si = spectra[j - m, at, :block], spectra[j - m, at, block:]
            return sums[0] + (fr * sr - fi * si), sums[1] + (fr * si + fi * sr)

        zero = jnp.zeros((tile, block), F32)
        re, im = lax.fori_loop(0, j + 1, term, (zero, zero))
        total[at, :block] = re
        total[at, block:] = im
        return carry

    lax.fori_loop(0, rows // tile, row_tile, 0)
    out_ref[...] = valid_part(total[...], both).astype(BF16)


def lead_kernel(shards, lead, me_ref, *refs):
    pieces = refs[:shards]
    filt_ref, table_ref, out_ref, spectra, signal, total = refs[shards:]
    me = me_ref[0]
    hi, lo, _, both = parts_of(table_ref)
    signal[0] = jnp.zeros(signal.shape[1:], BF16)
    for k in range(shards):
        signal[(me ^ k) + 1] = pieces[k][...]
    for j in range(shards):
        spectra[j] = window_spectrum(signal[j], signal[j + 1], hi, lo)
    one_block(me ^ lead, filt_ref, spectra, both, out_ref, total)


def long_kernel(shards, which, me_ref, filt_ref, spectra, table_ref, *refs):
    outs, sums = refs[:-1], refs[-1]
    rows, block = outs[0].shape
    me = me_ref[0]
    both = parts_of(table_ref)[3]
    tile = 8

    def body(i, carry):
        at = pl.ds(pl.multiple_of(i * tile, tile), tile)
        fr = [filt_ref[m, at, :block] for m in range(shards)]
        fi = [filt_ref[m, at, block:] for m in range(shards)]
        sr = [spectra[m, at, :block] for m in range(shards)]
        si = [spectra[m, at, block:] for m in range(shards)]
        for j in range(shards):
            re = fr[0] * sr[j] - fi[0] * si[j]
            im = fr[0] * si[j] + fi[0] * sr[j]
            for m in range(1, j + 1):
                re = re + (fr[m] * sr[j - m] - fi[m] * si[j - m])
                im = im + (fr[m] * si[j - m] + fi[m] * sr[j - m])
            sums[j, at, :block] = re
            sums[j, at, block:] = im
        return carry

    lax.fori_loop(0, rows // tile, body, 0)
    for k, out_ref in zip(which, outs):
        out_ref[...] = valid_part(sums[me ^ k], both).astype(BF16)


def last_kernel(order, me_ref, *refs):
    count = len(order)
    pieces, gates = refs[:count], refs[count : 2 * count]
    out_ref, made, sems = refs[2 * count :]
    rows = pieces[0].shape[0]
    me = me_ref[0]
    copies = []
    for i, k in enumerate(order):
        at = rows_at(me ^ k, rows)
        made[i] = (pieces[i][...].astype(F32) * gates[i][...].astype(F32)).astype(BF16)
        copies.append(pltpu.make_async_copy(made.at[i], out_ref.at[at, :], sems.at[i]))
        copies[-1].start()
    for copy in copies:
        copy.wait()


SMEM = pl.BlockSpec(memory_space=pltpu.SMEM)
VMEM = pl.BlockSpec(memory_space=pltpu.VMEM)
HBM = pl.BlockSpec(memory_space=pltpu.HBM)


def size_of(arrays):
    return sum(math.prod(a.shape) * a.dtype.itemsize for a in arrays)


def call(kernel, inputs, out_shape, scratch=(), flops=0, in_space=VMEM, out_space=VMEM, limit=28 * 2**20):
    moved = size_of(inputs)
    many = isinstance(out_shape, (list, tuple))
    return pl.pallas_call(
        kernel,
        out_shape=out_shape,
        in_specs=[SMEM if a.dtype == jnp.int32 else in_space for a in inputs],
        out_specs=[out_space] * len(out_shape) if many else out_space,
        scratch_shapes=list(scratch),
        compiler_params=pltpu.CompilerParams(vmem_limit_bytes=limit),
        cost_estimate=pl.CostEstimate(flops=flops, bytes_accessed=moved, transcendentals=0),
    )(*inputs)


def far_first(shards):
    order = []
    step = shards // 2
    while step:
        order += list(range(step, 2 * step))
        step //= 2
    return order


def stages(features, gate_one, taps_one, long_filter, skip_gain, taps_two, gate_two):
    shards = lax.axis_size(AXES)
    toks = lax.axis_size("tok")
    assert shards & (shards - 1) == 0
    assert lax.axis_size("grp") == 2 and lax.axis_size("sec") == 2
    channels, block = features.shape
    assert taps_one.shape[1] == block and taps_two.shape[1] == block
    narrow = channels // shards
    me = lax.axis_index(AXES)
    tok, sec, group = (lax.axis_index(name) for name in ("tok", "sec", "grp"))
    place = jnp.stack([me, tok, sec, group]).astype(jnp.int32)
    flops = 2 * channels * 256 * 256
    order = far_first(shards)
    lead = order[0]
    rest = order[1:] + [0]

    def swapped(piece, k):
        if k == 0:
            return piece
        return lax.ppermute(piece, AXES, [(i, i ^ k) for i in range(shards)])

    halo = lax.ppermute(features, AXES, [(i, i + 1) for i in range(shards - 1)])

    def rows_for(array, k):
        return lax.dynamic_slice_in_dim(array, (me ^ k) * narrow, narrow)

    table = tables(block)
    spectrum = jax.ShapeDtypeStruct((shards, narrow, 2 * block), F32)

    lags = [
        lax.dynamic_slice_in_dim(long_filter, ((tok ^ k) * 2 + group) * narrow, narrow)
        for k in range(toks)
    ]
    cuts = {k: [rows_for(a, k) for a in (features, gate_one, taps_one)] for k in range(shards)}
    skip_local, taps_local = rows_for(skip_gain, 0)[:, None], rows_for(taps_two, 0)
    lags, cuts, skip_local, taps_local = lax.optimization_barrier((lags, cuts, skip_local, taps_local))
    for k in range(1, toks):
        lags[k] = lax.ppermute(lags[k], "tok", [(i, i ^ k) for i in range(toks)])
    held = jnp.stack(lags)
    own_hat, taps_hat = call(
        functools.partial(prep_kernel, shards),
        (table, *[piece for k in range(shards) for piece in (cuts[k][0], cuts[k][2])]),
        [spectrum, spectrum],
        flops=2 * flops,
    )
    first = lax.ppermute(held, ("grp", "sec"), [(0, 2), (3, 1), (1, 0), (2, 3)])
    second = lax.ppermute(held, ("grp", "sec"), [(1, 2), (2, 1)])

    piece = jax.ShapeDtypeStruct((narrow, block), BF16)

    def operands(which):
        return (place, halo, table, own_hat, taps_hat, *[cuts[k][1] for k in which])

    (front,) = call(functools.partial(first_kernel, [lead]), operands([lead]), [piece], flops=flops)
    others = call(functools.partial(first_kernel, rest), operands(rest), [piece] * len(rest), flops=6 * flops)
    mixed = {k: swapped(p, k) for k, p in zip([lead] + rest, [front] + list(others))}

    gate_late, _ = lax.optimization_barrier((gate_two, others[0]))
    joined = call(
        functools.partial(filter_kernel, toks),
        (place, held, first, second, taps_local, skip_local, table),
        spectrum,
        scratch=[
            pltpu.VMEM((shards + 1, narrow, block), BF16),
            pltpu.VMEM((narrow, 2 * block), F32),
        ],
        flops=6 * flops,
    )
    front, spectra = call(
        functools.partial(lead_kernel, shards, lead),
        (place, *[mixed[k] for k in range(shards)], joined, table),
        [piece, spectrum],
        scratch=[
            pltpu.VMEM((shards + 1, narrow, block), BF16),
            pltpu.VMEM((narrow, 2 * block), F32),
        ],
        flops=3 * flops,
    )
    others = call(
        functools.partial(long_kernel, shards, rest),
        (place, joined, spectra, table),
        [piece] * len(rest),
        scratch=[pltpu.VMEM((shards, narrow, 2 * block), F32)],
        flops=3 * flops,
    )
    result = {k: swapped(p, k) for k, p in zip([lead] + rest, [front] + list(others))}
    ready = [0] + order[::-1]
    return call(
        functools.partial(last_kernel, ready),
        (place, *[result[k] for k in ready], *[rows_for(gate_late, k) for k in ready]),
        jax.ShapeDtypeStruct((channels, block), BF16),
        scratch=[
            pltpu.VMEM((shards, narrow, block), BF16),
            pltpu.SemaphoreType.DMA((shards,)),
        ],
        flops=channels * block,
        out_space=HBM,
    )


def solution(mesh):
    in_specs = (
        P("ch", ("grp", "tok", "sec")),
        P("ch", ("grp", "tok", "sec")),
        P("ch", None),
        P("ch", ("tok", "sec")),
        P("ch"),
        P("ch", None),
        P("ch", ("grp", "tok", "sec")),
    )
    out_specs = P("ch", ("grp", "tok", "sec"))
    return jax.shard_map(stages, mesh=mesh, in_specs=in_specs, out_specs=out_specs, check_vma=False)
```

```python
import functools
import math

import jax
import jax.numpy as jnp
import numpy as np
from jax import lax
from jax.experimental import pallas as pl
from jax.experimental.pallas import tpu as pltpu
from jax.sharding import PartitionSpec as P


AXES = ("tok", "sec")
F32 = jnp.float32
BF16 = jnp.bfloat16


def split_const(matrix):
    hi = matrix.astype(np.float32).astype(jnp.bfloat16)
    lo = (matrix - hi.astype(np.float64)).astype(np.float32).astype(jnp.bfloat16)
    return hi, lo


def tables(block):
    length = 2 * block
    sample = np.arange(length)[:, None]
    freq = np.arange(block)[None, :]
    turns = (sample * (2 * freq + 1)) % (2 * length)
    angle = turns * (math.pi / length)
    forward = np.concatenate([np.cos(angle), -np.sin(angle)], axis=1)
    hi, lo = split_const(forward)
    top = np.concatenate([hi[:block], lo[:block]], axis=0)
    back = forward[block:].T / block
    back_hi, back_lo = split_const(back)
    both = np.concatenate([back_hi, back_lo], axis=1)
    return jnp.asarray(np.concatenate([hi, lo, top, both], axis=0))


def parts_of(table_ref):
    n = table_ref.shape[1]
    return tuple(table_ref[i * n : (i + 1) * n, :] for i in range(4))


def mm(left, right):
    return jnp.dot(left, right, preferred_element_type=F32)


def window_spectrum(before, here, hi, lo):
    window = jnp.concatenate([before, here], axis=1)
    return mm(window, hi) + mm(window, lo)


def block_spectrum(rows, top):
    return mm(jnp.concatenate([rows, rows], axis=1), top)


def two_parts(value):
    hi = value.astype(BF16)
    return hi, (value - hi.astype(F32)).astype(BF16)


def times(left, right):
    n = left.shape[-1] // 2
    lr, li, rr, ri = left[:, :n], left[:, n:], right[:, :n], right[:, n:]
    return jnp.concatenate([lr * rr - li * ri, lr * ri + li * rr], axis=1)


def valid_part(spectrum, both):
    n = both.shape[1] // 2
    hi, lo = two_parts(spectrum)
    wide = mm(hi, both)
    return wide[:, :n] + wide[:, n:] + mm(lo, both[:, :n])


def position():
    return lax.axis_index("tok") * lax.axis_size("sec") + lax.axis_index("sec")


def rows_at(index, rows):
    return pl.ds(pl.multiple_of(index * rows, rows), rows)


def prep_kernel(shards, table_ref, *refs):
    own_hat, taps_hat = refs[2 * shards :]
    hi, lo, top, _ = parts_of(table_ref)
    n = hi.shape[0] // 2
    bottom = jnp.concatenate([hi[n:], lo[n:]], axis=0)
    for k in range(shards):
        own_hat[k] = block_spectrum(refs[2 * k][...], bottom)
        taps_hat[k] = block_spectrum(refs[2 * k + 1][...], top)


def first_kernel(which, halo_ref, table_ref, own_hat, taps_hat, *refs):
    count = len(which)
    gates, outs = refs[:count], refs[count:]
    rows = outs[0].shape[0]
    me = position()
    _, _, top, both = parts_of(table_ref)
    for i, k in enumerate(which):
        spectrum = own_hat[k] + block_spectrum(halo_ref[rows_at(me ^ k, rows), :], top)
        conv = valid_part(times(spectrum, taps_hat[k]), both)
        outs[i][...] = (conv * gates[i][...].astype(F32)).astype(BF16)


def filter_kernel(toks, held0_ref, first0_ref, second0_ref, held_ref, first_ref, second_ref, taps_ref, skip_ref, table_ref, out_ref, lags, taps_hat):
    tok, sec, group = (lax.axis_index(name) for name in ("tok", "sec", "grp"))
    hi, lo, top, both = parts_of(table_ref)
    lags[0] = jnp.zeros(lags.shape[1:], BF16)

    def fill(same0_ref, other0_ref, same_ref, other_ref):
        for k in range(toks):
            at = (tok ^ k) * 2 + 1
            lags[at + sec] = same_ref[k - 1] if k else same0_ref[...]
            lags[at + 1 - sec] = other_ref[k - 1] if k else other0_ref[...]

    @pl.when(sec == group)
    def _():
        fill(held0_ref, first0_ref, held_ref, first_ref)

    @pl.when(sec != group)
    def _():
        fill(first0_ref, second0_ref, first_ref, second_ref)

    taps_hat[...] = block_spectrum(taps_ref[...], top)
    for m in range(2 * toks):
        spectrum = window_spectrum(lags[m], lags[m + 1], hi, lo)
        joined = valid_part(times(spectrum, taps_hat[...]), both)
        part_hi, part_lo = two_parts(joined)
        n = part_hi.shape[1]
        result = block_spectrum(part_hi, top) + mm(part_lo, top[:n])
        if m == 0:
            result = result + skip_ref[...] * taps_hat[...]
        out_ref[m] = result


def some_blocks(which, shards, me, filt_ref, spectra, sums):
    rows, block = filt_ref.shape[1], filt_ref.shape[2] // 2
    tile = 8
    for place in range(shards):

        @pl.when(me == place)
        def _():
            blocks = [place ^ k for k in which]
            count = max(blocks) + 1

            def body(i, carry):
                at = pl.ds(pl.multiple_of(i * tile, tile), tile)
                fr = [filt_ref[m, at, :block] for m in range(count)]
                fi = [filt_ref[m, at, block:] for m in range(count)]
                sr = [spectra[m, at, :block] for m in range(count)]
                si = [spectra[m, at, block:] for m in range(count)]
                for slot, j in enumerate(blocks):
                    re = fr[0] * sr[j] - fi[0] * si[j]
                    im = fr[0] * si[j] + fi[0] * sr[j]
                    for m in range(1, j + 1):
                        re = re + (fr[m] * sr[j - m] - fi[m] * si[j - m])
                        im = im + (fr[m] * si[j - m] + fi[m] * sr[j - m])
                    sums[slot, at, :block] = re
                    sums[slot, at, block:] = im
                return carry

            lax.fori_loop(0, rows // tile, body, 0)


def lead_kernel(shards, which, *refs):
    pieces = refs[:shards]
    filt_ref, table_ref, spectra = refs[shards : shards + 3]
    outs, (signal, sums) = refs[shards + 3 : -2], refs[-2:]
    me = position()
    hi, lo, _, both = parts_of(table_ref)
    signal[0] = jnp.zeros(signal.shape[1:], BF16)
    for k in range(shards):
        signal[(me ^ k) + 1] = pieces[k][...]
    for j in range(shards):
        spectra[j] = window_spectrum(signal[j], signal[j + 1], hi, lo)
    some_blocks(which, shards, me, filt_ref, spectra, sums)
    for slot, out_ref in enumerate(outs):
        out_ref[...] = valid_part(sums[slot], both).astype(BF16)


def long_kernel(shards, which, filt_ref, spectra, table_ref, *refs):
    outs, sums = refs[:-1], refs[-1]
    rows, block = outs[0].shape
    me = position()
    both = parts_of(table_ref)[3]
    tile = 8

    def body(i, carry):
        at = pl.ds(pl.multiple_of(i * tile, tile), tile)
        fr = [filt_ref[m, at, :block] for m in range(shards)]
        fi = [filt_ref[m, at, block:] for m in range(shards)]
        sr = [spectra[m, at, :block] for m in range(shards)]
        si = [spectra[m, at, block:] for m in range(shards)]
        for j in range(shards):
            re = fr[0] * sr[j] - fi[0] * si[j]
            im = fr[0] * si[j] + fi[0] * sr[j]
            for m in range(1, j + 1):
                re = re + (fr[m] * sr[j - m] - fi[m] * si[j - m])
                im = im + (fr[m] * si[j - m] + fi[m] * sr[j - m])
            sums[j, at, :block] = re
            sums[j, at, block:] = im
        return carry

    lax.fori_loop(0, rows // tile, body, 0)
    for k, out_ref in zip(which, outs):
        out_ref[...] = valid_part(sums[me ^ k], both).astype(BF16)


def last_kernel(order, *refs):
    count = len(order)
    pieces, gates = refs[:count], refs[count : 2 * count]
    out_ref, made, sems = refs[2 * count :]
    rows = pieces[0].shape[0]
    me = position()
    copies = []
    for i, k in enumerate(order):
        at = rows_at(me ^ k, rows)
        made[i] = (pieces[i][...].astype(F32) * gates[i][...].astype(F32)).astype(BF16)
        copies.append(pltpu.make_async_copy(made.at[i], out_ref.at[at, :], sems.at[i]))
        copies[-1].start()
    for copy in copies:
        copy.wait()


VMEM = pl.BlockSpec(memory_space=pltpu.VMEM)
HBM = pl.BlockSpec(memory_space=pltpu.HBM)


def size_of(arrays):
    return sum(math.prod(a.shape) * a.dtype.itemsize for a in arrays)


def call(kernel, inputs, out_shape, scratch=(), flops=0, in_space=VMEM, out_space=VMEM, limit=28 * 2**20):
    moved = size_of(inputs)
    many = isinstance(out_shape, (list, tuple))
    return pl.pallas_call(
        kernel,
        out_shape=out_shape,
        in_specs=[in_space] * len(inputs),
        out_specs=[out_space] * len(out_shape) if many else out_space,
        scratch_shapes=list(scratch),
        compiler_params=pltpu.CompilerParams(vmem_limit_bytes=limit),
        cost_estimate=pl.CostEstimate(flops=flops, bytes_accessed=moved, transcendentals=0),
    )(*inputs)


def far_first(shards):
    order = []
    step = shards // 2
    while step:
        order += list(range(step, 2 * step))
        step //= 2
    return order


def stages(features, gate_one, taps_one, long_filter, skip_gain, taps_two, gate_two):
    shards = lax.axis_size(AXES)
    toks = lax.axis_size("tok")
    assert shards & (shards - 1) == 0
    assert lax.axis_size("grp") == 2 and lax.axis_size("sec") == 2
    channels, block = features.shape
    assert taps_one.shape[1] == block and taps_two.shape[1] == block
    narrow = channels // shards
    me = position()
    tok, _, group = (lax.axis_index(name) for name in ("tok", "sec", "grp"))
    flops = 2 * channels * 256 * 256
    order = far_first(shards)
    lead = order[0]
    rest = order[1:] + [0]

    def swapped(piece, k):
        if k == 0:
            return piece
        return lax.ppermute(piece, AXES, [(i, i ^ k) for i in range(shards)])

    halo = lax.ppermute(features, AXES, [(i, i + 1) for i in range(shards - 1)])

    def rows_for(array, k):
        return lax.dynamic_slice_in_dim(array, (me ^ k) * narrow, narrow)

    table = tables(block)
    spectrum = jax.ShapeDtypeStruct((shards, narrow, 2 * block), F32)

    lags = [
        lax.dynamic_slice_in_dim(long_filter, ((tok ^ k) * 2 + group) * narrow, narrow)
        for k in range(toks)
    ]
    cuts = {k: [rows_for(a, k) for a in (features, gate_one, taps_one)] for k in range(shards)}
    skip_local, taps_local = rows_for(skip_gain, 0)[:, None], rows_for(taps_two, 0)
    lags, cuts, skip_local, taps_local = lax.optimization_barrier((lags, cuts, skip_local, taps_local))
    for k in range(1, toks):
        lags[k] = lax.ppermute(lags[k], "tok", [(i, i ^ k) for i in range(toks)])
    held = jnp.stack(lags[1:])
    own_hat, taps_hat = call(
        functools.partial(prep_kernel, shards),
        (table, *[piece for k in range(shards) for piece in (cuts[k][0], cuts[k][2])]),
        [spectrum, spectrum],
        flops=2 * flops,
    )

    def across(array):
        first = lax.ppermute(array, ("grp", "sec"), [(0, 2), (3, 1), (1, 0), (2, 3)])
        second = lax.ppermute(array, ("grp", "sec"), [(1, 2), (2, 1)])
        return array, first, second

    parities = across(lags[0]) + across(held)

    piece = jax.ShapeDtypeStruct((narrow, block), BF16)

    def operands(which):
        return (halo, table, own_hat, taps_hat, *[cuts[k][1] for k in which])

    (front,) = call(functools.partial(first_kernel, [lead]), operands([lead]), [piece], flops=flops)
    others = call(functools.partial(first_kernel, rest), operands(rest), [piece] * len(rest), flops=6 * flops)
    mixed = {k: swapped(p, k) for k, p in zip([lead] + rest, [front] + list(others))}

    gate_late, _ = lax.optimization_barrier((gate_two, others[0]))
    joined = call(
        functools.partial(filter_kernel, toks),
        (*parities, taps_local, skip_local, table),
        spectrum,
        scratch=[
            pltpu.VMEM((shards + 1, narrow, block), BF16),
            pltpu.VMEM((narrow, 2 * block), F32),
        ],
        flops=6 * flops,
    )
    leads = order[:1]
    others = order[1:] + [0]
    spectra, *made = call(
        functools.partial(lead_kernel, shards, leads),
        (*[mixed[k] for k in range(shards)], joined, table),
        [spectrum] + [piece] * len(leads),
        scratch=[
            pltpu.VMEM((shards + 1, narrow, block), BF16),
            pltpu.VMEM((len(leads), narrow, 2 * block), F32),
        ],
        flops=3 * flops,
    )
    made += call(
        functools.partial(long_kernel, shards, others),
        (joined, spectra, table),
        [piece] * len(others),
        scratch=[pltpu.VMEM((shards, narrow, 2 * block), F32)],
        flops=3 * flops,
    )
    result = {k: swapped(p, k) for k, p in zip(leads + others, made)}
    ready = [0] + order[::-1]
    return call(
        functools.partial(last_kernel, ready),
        (*[result[k] for k in ready], *[rows_for(gate_late, k) for k in ready]),
        jax.ShapeDtypeStruct((channels, block), BF16),
        scratch=[
            pltpu.VMEM((shards, narrow, block), BF16),
            pltpu.SemaphoreType.DMA((shards,)),
        ],
        flops=channels * block,
        out_space=HBM,
    )


def solution(mesh):
    in_specs = (
        P("ch", ("grp", "tok", "sec")),
        P("ch", ("grp", "tok", "sec")),
        P("ch", None),
        P("ch", ("tok", "sec")),
        P("ch"),
        P("ch", None),
        P("ch", ("grp", "tok", "sec")),
    )
    out_specs = P("ch", ("grp", "tok", "sec"))
    return jax.shard_map(stages, mesh=mesh, in_specs=in_specs, out_specs=out_specs, check_vma=False)
```
